32 devices in a mesh: cuts: 16 (over z, x, core), ang: 2 (over y).
Axes of the slice: x: 2, y: 2, z: 4, core: 2. Of those that a mesh axis runs over, the one named last changes fastest.
Arguments:
- projections: bfloat16 [16, 16, 2, 128, 256], P('cuts', None, 'ang'), may hold values from -48 to 48
- start_image: bfloat16 [4096, 1024], P('cuts'), may hold values from 0 to 2
- system: bfloat16 [8, 16, 2, 64, 128], P('ang'), may hold values from 0.0009994507 to 0.029907227
- first_tile: int32 [8, 16], P('ang'), may hold values from 0 to 3, as said below
Outputs:
- new_image: float32 [4096, 1024], P('cuts', 'ang')
- residual: bfloat16 [16, 4096, 256], P('ang', 'cuts')
The draws below stay inside these ranges and needn't reach their ends.
Inputs may be any that keep to these rules, and one draw needn't show every extreme that they name: In every angle block each bin tile is first_tile of at least one pixel tile; every pixel tile meets exactly two bin tiles, first_tile and first_tile + 1 modulo 4.
All inputs are finite; a program needn't handle non-finite values.
Results may differ from the reference program's by a relative error of at most 0.001.
Values may be sent and summed in bfloat16 or wider, within the bound.
A program may use at most 128 MiB of HBM per device.

```python
import jax
import jax.numpy as jnp
from jax import lax

TILE_WIDTH = 64
PAIR_ANG = 2
BIN_TILE_COUNT = 4
PIXEL_TILES = 16
ANGLE_COUNT = 16
BLOCKS = 8
ROWS = 4096
SLICE_BLOCKS = 16
ROW_GROUPS = 2
GROUP_SLICES = 128
NPIX = 1024
DETECTOR_BINS = 256


def draw_first_tile(key, part):
    base_key = jax.random.fold_in(key, 31)
    order_key = jax.random.fold_in(key, 47)
    base = jax.random.randint(base_key, (BLOCKS, PIXEL_TILES), 0, BIN_TILE_COUNT, dtype=jnp.int32)

    def one_order(subkey):
        return jax.random.permutation(subkey, PIXEL_TILES)
    orders = jax.vmap(one_order)(jax.random.split(order_key, BLOCKS))
    ranks = jnp.argsort(orders, axis=1, stable=True).astype(jnp.int32)
    return jnp.where(ranks < BIN_TILE_COUNT, ranks, base).astype(jnp.int32)


def levels(rng, shape, cuts, least, high):
    def one(dim, shards_of):
        draws = jax.random.uniform(jax.random.fold_in(jax.random.fold_in(rng, 6), dim), (shards_of,), jnp.float32, least / len(cuts), high / len(cuts))
        return jnp.repeat(jnp.exp(draws), shape[dim] // shards_of).reshape((-1,) + (1,) * (len(shape) - dim - 1))

    factor_of = one(*cuts[0])
    for cut in cuts[1:]:
        factor_of = factor_of * one(*cut)
    return factor_of


def scatter_about(stream_key, shape, spread, bound, cuts=(), kind=jnp.bfloat16):
    level = levels(stream_key, shape, cuts, -0.22, 0.18) if cuts else 1.0
    result = jax.random.normal(stream_key, shape, jnp.float32) * spread * level
    return jnp.minimum(jnp.maximum(result, -bound), bound).astype(kind)


def setup_inputs(seed: int = 0) -> dict:
    key_of = jax.random.split(jax.random.key(seed), 5)
    return {
        "projections": scatter_about(key_of[0], (ANGLE_COUNT, SLICE_BLOCKS, ROW_GROUPS, GROUP_SLICES, DETECTOR_BINS), (0.031 * TILE_WIDTH * PIXEL_TILES / BIN_TILE_COUNT), 48.0, ((0, 16), (2, 2))),
        "start_image": jnp.clip(2.0 * jax.random.uniform(key_of[1], (ROWS, NPIX), jnp.float32) ** levels(key_of[1], (ROWS, NPIX), ((0, 16),), -0.2, 0.2), 0.0, 2.0).astype(jnp.bfloat16),
        "system": jnp.clip(0.0009994507 + 0.028907776 * jax.random.uniform(key_of[2], (BLOCKS, PIXEL_TILES, 2, TILE_WIDTH, PAIR_ANG * TILE_WIDTH), jnp.float32) ** levels(key_of[2], (BLOCKS, PIXEL_TILES, 2, TILE_WIDTH, PAIR_ANG * TILE_WIDTH), ((0, 2),), -0.2, 0.2), 0.0009994507, 0.029907227).astype(jnp.bfloat16),
        "first_tile": draw_first_tile(jax.random.fold_in(key_of[4], 71), 0),
    }


def reference(projections, start_image, system, first_tile):
    sinogram = projections.reshape(BLOCKS, PAIR_ANG, ROWS, DETECTOR_BINS)
    pixels = start_image.astype(jnp.float32).reshape(ROWS, PIXEL_TILES, TILE_WIDTH)
    tile_ids = jnp.arange(BIN_TILE_COUNT, dtype=jnp.int32)
    highest = lax.Precision.HIGHEST

    def step_block(carry, inputs):
        backproj, col_total = carry
        weights, first, measured = inputs
        weights = weights.astype(jnp.float32)
        bin_index = jnp.stack([first, (first + 1) % BIN_TILE_COUNT], axis=1)
        onehot = (bin_index[:, :, None] == tile_ids).astype(jnp.float32)
        partial_value = jnp.einsum('rpi,pjic->pjrc', pixels, weights, precision=highest)
        forward = jnp.einsum('pjb,pjrc->brc', onehot, partial_value, precision=highest)
        row_total = jnp.einsum('pjb,pjc->bc', onehot, jnp.sum(weights, axis=2), precision=highest)
        measured_t = measured.astype(jnp.float32).reshape(PAIR_ANG, ROWS, BIN_TILE_COUNT, TILE_WIDTH)
        measured_t = measured_t.transpose(2, 1, 0, 3).reshape(BIN_TILE_COUNT, ROWS, PAIR_ANG * TILE_WIDTH)
        resid = ((measured_t - forward) / row_total[:, None, :]).astype(jnp.bfloat16)
        resid = lax.optimization_barrier(resid)
        picked = jnp.einsum('pjb,brc->pjrc', onehot, resid.astype(jnp.float32), precision=highest)
        backproj = backproj + jnp.einsum('pjrc,pjic->rpi', picked, weights, precision=highest)
        col_total = col_total + jnp.sum(weights, axis=(1, 3))
        out_block = resid.reshape(BIN_TILE_COUNT, ROWS, PAIR_ANG, TILE_WIDTH).transpose(2, 1, 0, 3).reshape(PAIR_ANG, ROWS, DETECTOR_BINS)
        return (backproj, col_total), out_block

    start = (jnp.zeros((ROWS, PIXEL_TILES, TILE_WIDTH), jnp.float32), jnp.zeros((PIXEL_TILES, TILE_WIDTH), jnp.float32))
    (backproj, col_total), blocks_out = lax.scan(step_block, start, (system, first_tile, sinogram))
    residual = blocks_out.reshape(ANGLE_COUNT, ROWS, DETECTOR_BINS)
    new_image = start_image.astype(jnp.float32) + (backproj / col_total[None, :, :]).reshape(ROWS, NPIX)
    return new_image, residual
```

```python
import functools

import jax
import jax.numpy as jnp
from jax import lax
from jax.experimental import pallas as pl
from jax.experimental.pallas import tpu as pltpu
from jax.sharding import PartitionSpec as P

MESH = pl.DeviceIdType.MESH
NT = (((1,), (1,)), ((), ()))
MAX_CHUNKS = 4


def kernel(
    C, G, NC, first, proj, image, system, new_out, res_out,
    img, sysv, A, F, inv, hop, arr, R, U, own, urecv, colp, crecv, newv,
    img_sem, sys_sem, send_sem, hop_sem, fwd_sem, arr_sem,
    usend_sem, urecv_sem, csend_sem, crecv_sem, res_sem, new_sem,
):
    c = lax.axis_index("cuts")
    a = lax.axis_index("ang")
    T = C // G
    blocks, ptiles, _, W, PW = system.shape
    KR = proj.shape[3]
    kc = KR // NC
    rows = G * kc
    npix = image.shape[1]
    share = npix // G
    bins = proj.shape[4]
    half = bins // PW
    ntiles = bins // W

    barrier = pltpu.get_barrier_semaphore()
    for s in range(1, C):
        pl.semaphore_signal(barrier, inc=1, device_id=(lax.rem(c + s, C), a), device_id_type=MESH)
    for s in range(1, G):
        pl.semaphore_signal(barrier, inc=1, device_id=(c, lax.rem(a + s, G)), device_id_type=MESH)

    sys_copy = pltpu.make_async_copy(system, sysv, sys_sem)
    sys_copy.start()
    img_copies = []
    for q in range(NC):
        for b in range(G):
            cp = pltpu.make_async_copy(
                image.at[pl.ds(b * KR + q * kc, kc)], img.at[q, b], img_sem.at[q, b]
            )
            cp.start()
            img_copies.append(cp)
    for q in range(NC):
        pltpu.make_async_copy(
            proj.at[0, c, 0, pl.ds(q * kc, kc)], hop.at[q, c], hop_sem.at[q]
        ).start()

    pl.semaphore_wait(barrier, C - 1 + G - 1)

    for q in range(NC):
        for s in range(1, C):
            o = lax.rem(c + s, C)
            pltpu.make_async_remote_copy(
                src_ref=proj.at[0, o, 0, pl.ds(q * kc, kc)],
                dst_ref=hop.at[q, c],
                send_sem=send_sem,
                recv_sem=hop_sem.at[q],
                device_id=(o, a),
                device_id_type=MESH,
            ).start()

    sys_copy.wait()


    def build(p, carry):
        rows_p = pl.ds(pl.multiple_of(p * W, W), W)
        for g in range(blocks):
            f = first[g, p]
            w = [sysv[g, p, j].astype(jnp.float32) for j in range(2)]
            r = [pltpu.roll(x, W, 1) for x in w]
            up = (lax.broadcasted_iota(jnp.int32, (W, PW), 1) // W)
            for t in range(PW // W):
                x = [jnp.where(up == t, w[j], r[j]) for j in range(2)]
                for h in range(half):
                    b = up + h * (PW // W)
                    second = lax.rem(f + 1, ntiles)
                    tile = jnp.where(b == f, x[0], jnp.where(b == second, x[1], 0.0))
                    A[g * (PW // W) + t, rows_p, pl.ds(h * PW, PW)] = tile.astype(jnp.bfloat16)
        return carry

    lax.fori_loop(0, ptiles, build, 0)

    colp[...] = jnp.zeros_like(colp)
    for cp in img_copies:
        cp.wait()

    def project(t, carry):
        m = A[t]
        F[t] = jnp.dot(
            img[...].reshape(NC * rows, npix), m, preferred_element_type=jnp.float32
        )
        ones_r = jnp.ones((16, npix), jnp.bfloat16)
        ones_b = jnp.ones((16, bins), jnp.bfloat16)
        inv[t] = 1.0 / jnp.dot(ones_r, m, preferred_element_type=jnp.float32)[:8]
        for g in range(G):
            colp[g] += lax.dot_general(
                ones_b, A[t, pl.ds(g * share, share)], NT, preferred_element_type=jnp.float32
            )[:8]
        return carry

    lax.fori_loop(0, T, project, 0)

    for s in range(1, G):
        g = lax.rem(a + s, G)
        pltpu.make_async_remote_copy(
            src_ref=colp.at[g], dst_ref=crecv.at[s - 1], send_sem=csend_sem.at[s - 1],
            recv_sem=crecv_sem, device_id=(c, g), device_id_type=MESH,
        ).start()

    def forward_on(q):
        pltpu.make_async_copy(hop.at[q], hop.at[q], hop_sem.at[q]).wait()
        for s in range(1, G):
            g = lax.rem(a + s, G)
            pltpu.make_async_remote_copy(
                src_ref=hop.at[q, pl.ds(g * T, T)],
                dst_ref=arr.at[q, s - 1],
                send_sem=fwd_sem.at[q, s - 1],
                recv_sem=arr_sem.at[q, s - 1],
                device_id=(c, g),
                device_id_type=MESH,
            ).start()

    def res_copies(q):
        out = []
        for b in range(G):
            out.append(pltpu.make_async_copy(
                R.at[q, :, b], res_out.at[:, pl.ds(b * KR + q * kc, kc)], res_sem.at[q, b]
            ))
        return out

    def new_copies(q):
        return [
            pltpu.make_async_copy(
                newv.at[q, b], new_out.at[pl.ds(b * KR + q * kc, kc)], new_sem.at[q, b]
            )
            for b in range(G)
        ]

    def residual_part(q, b, source):
        def body(t, carry):
            value = source(t).astype(jnp.float32)
            f = F[t, pl.ds(pl.multiple_of(q * rows + b * kc, kc), kc)]
            R[q, t, b] = ((value - f) * inv[t][:1]).astype(jnp.bfloat16)
            return carry

        lax.fori_loop(0, T, body, 0)

    def back(q, g):
        total = jnp.zeros((rows, share), jnp.float32)
        pix = pl.ds(pl.multiple_of(g * share, share), share)
        for t in range(T):
            total = total + lax.dot_general(
                R[q, t].reshape(rows, bins), A[t, pix], NT, preferred_element_type=jnp.float32
            )
        return total

    def u_copy(q, s):
        g = lax.rem(a + s, G)
        return pltpu.make_async_remote_copy(
            src_ref=U.at[q, s - 1], dst_ref=urecv.at[q, s - 1],
            send_sem=usend_sem.at[q, s - 1], recv_sem=urecv_sem.at[q, s - 1],
            device_id=(c, g), device_id_type=MESH,
        )

    def process(q):
        residual_part(q, a, lambda t: hop[q, a * T + t])
        for s in range(1, G):
            pltpu.make_async_copy(arr.at[q, s - 1], arr.at[q, s - 1], arr_sem.at[q, s - 1]).wait()
            residual_part(q, lax.rem(a + G - s, G), lambda t, s=s: arr[q, s - 1, t])
        for cp in res_copies(q):
            cp.start()
        for s in range(1, G):
            U[q, s - 1] = back(q, lax.rem(a + s, G))
            u_copy(q, s).start()
        own[q] = back(q, a)

    def finish(q):
        total = own[q]
        for s in range(1, G):
            u_copy(q, s).wait_recv()
            total = total + urecv[q, s - 1]
        mine = img[q, :, :, pl.ds(pl.multiple_of(a * share, share), share)]
        new = mine.reshape(rows, share).astype(jnp.float32) + total * own_inv
        newv[q] = new.reshape(G, kc, share)
        for cp in new_copies(q):
            cp.start()

    forward_on(0)
    pltpu.make_async_copy(crecv, crecv, crecv_sem).wait()
    columns = colp[a][:1]
    for s in range(1, G):
        columns = columns + crecv[s - 1][:1]
    own_inv = 1.0 / columns
    for q in range(NC):
        process(q)
        if q + 1 < NC:
            forward_on(q + 1)
        if q >= 1:
            finish(q - 1)
    finish(NC - 1)

    pltpu.make_async_copy(
        proj.at[0, pl.ds(0, C - 1)], proj.at[0, pl.ds(0, C - 1)], send_sem
    ).wait()
    for s in range(1, G):
        pltpu.make_async_remote_copy(
            src_ref=colp.at[0], dst_ref=crecv.at[s - 1], send_sem=csend_sem.at[s - 1],
            recv_sem=crecv_sem, device_id=(c, lax.rem(a + s, G)), device_id_type=MESH,
        ).wait_send()
    for q in range(NC):
        for s in range(1, G):
            u_copy(q, s).wait_send()
            pltpu.make_async_copy(
                hop.at[q, pl.ds(0, T)], hop.at[q, pl.ds(0, T)], fwd_sem.at[q, s - 1]
            ).wait()
        for cp in res_copies(q) + new_copies(q):
            cp.wait()


def on_device(C, G, projections, start_image, system, first_tile):
    T = C // G
    KR = projections.shape[3]
    NC = max(1, min(MAX_CHUNKS, KR // 16))
    kc = KR // NC
    rows = G * kc
    slices, npix = start_image.shape
    bins = projections.shape[4]
    share = npix // G
    bf16, f32 = jnp.bfloat16, jnp.float32
    dma = pltpu.SemaphoreType.DMA
    hbm = pl.BlockSpec(memory_space=pl.ANY)
    return pl.pallas_call(
        functools.partial(kernel, C, G, NC),
        out_shape=(
            jax.ShapeDtypeStruct((slices, share), f32),
            jax.ShapeDtypeStruct((T, slices, bins), bf16),
        ),
        in_specs=[pl.BlockSpec(memory_space=pltpu.SMEM), hbm, hbm, hbm],
        out_specs=(hbm, hbm),
        scratch_shapes=[
            pltpu.VMEM((NC, G, kc, npix), bf16),
            pltpu.VMEM(system.shape, bf16),
            pltpu.VMEM((T, npix, bins), bf16),
            pltpu.VMEM((T, NC * rows, bins), f32),
            pltpu.VMEM((T, 8, bins), f32),
            pltpu.VMEM((NC, C, kc, bins), bf16),
            pltpu.VMEM((NC, G - 1, T, kc, bins), bf16),
            pltpu.VMEM((NC, T, G, kc, bins), bf16),
            pltpu.VMEM((NC, G - 1, rows, share), f32),
            pltpu.VMEM((NC, rows, share), f32),
            pltpu.VMEM((NC, G - 1, rows, share), f32),
            pltpu.VMEM((G, 8, share), f32),
            pltpu.VMEM((G - 1, 8, share), f32),
            pltpu.VMEM((NC, G, kc, share), f32),
            dma((NC, G)),
            dma,
            dma,
            dma((NC,)),
            dma((NC, G - 1)),
            dma((NC, G - 1)),
            dma((NC, G - 1)),
            dma((NC, G - 1)),
            dma((G - 1,)),
            dma,
            dma((NC, G)),
            dma((NC, G)),
        ],
        compiler_params=pltpu.CompilerParams(
            collective_id=0, has_side_effects=True, vmem_limit_bytes=48 * 1024 * 1024
        ),
    )(first_tile, projections, start_image, system)


def solution(mesh):
    in_specs = (
        P("cuts", None, "ang", None, None),
        P("cuts", None),
        P("ang", None, None, None, None),
        P("ang", None),
    )
    out_specs = (P("cuts", "ang"), P("ang", "cuts", None))
    return jax.shard_map(
        functools.partial(on_device, mesh.shape["cuts"], mesh.shape["ang"]),
        mesh=mesh, in_specs=in_specs, out_specs=out_specs, check_vma=False,
    )
```

```python
import functools

import jax
import jax.numpy as jnp
from jax import lax
from jax.experimental import pallas as pl
from jax.experimental.pallas import tpu as pltpu
from jax.sharding import PartitionSpec as P

MESH = pl.DeviceIdType.MESH
NT = (((1,), (1,)), ((), ()))
MAX_CHUNKS = 4


def kernel(
    C, G, NC, first_in, proj, image, system, new_out, res_out,
    first, img, sysv, A, F, inv, arr, R, U, own, urecv, colp, crecv, newv,
    first_sem, img_sem, sys_sem, send_sem, arr_sem,
    usend_sem, urecv_sem, csend_sem, crecv_sem, res_sem, new_sem,
):
    c = lax.axis_index("cuts")
    a = lax.axis_index("ang")
    T = C // G
    blocks, ptiles, _, W, PW = system.shape
    KR = proj.shape[3]
    kc = KR // NC
    rows = G * kc
    npix = image.shape[1]
    share = npix // G
    bins = proj.shape[4]
    half = bins // PW
    ntiles = bins // W

    tgt = c // T
    slot = a * T + lax.rem(c, T)

    barrier = pltpu.get_barrier_semaphore()
    for i in range(T):
        source = a * T + lax.rem(c + i, T)
        for s in range(1 if i == 0 else 0, G):
            pl.semaphore_signal(
                barrier, inc=1, device_id=(source, lax.rem(a + s, G)), device_id_type=MESH
            )

    @pl.when(tgt != a)
    def _():
        pl.semaphore_signal(
            barrier, inc=1, device_id=(a * T + lax.rem(c, T), a), device_id_type=MESH
        )

    for s in range(1, G):
        pl.semaphore_signal(barrier, inc=1, device_id=(c, lax.rem(a + s, G)), device_id_type=MESH)

    sys_copy = pltpu.make_async_copy(system, sysv, sys_sem)
    sys_copy.start()
    first_copy = pltpu.make_async_copy(first_in, first, first_sem)
    first_copy.start()
    img_copies = []
    for q in range(NC):
        for b in range(G):
            cp = pltpu.make_async_copy(
                image.at[pl.ds(b * KR + q * kc, kc)], img.at[q, b], img_sem.at[q, b]
            )
            cp.start()
            img_copies.append(cp)
    pl.semaphore_wait(barrier, C + G - 1 - jnp.where(tgt == a, 1, 0))

    def piece(q, o):
        return pltpu.make_async_remote_copy(
            src_ref=proj.at[0, o, 0, pl.ds(q * kc, kc)],
            dst_ref=arr.at[q, slot],
            send_sem=send_sem,
            recv_sem=arr_sem.at[q],
            device_id=(o, tgt),
            device_id_type=MESH,
        )

    for q in range(NC):
        for s in range(1, C):
            piece(q, lax.rem(c + s, C)).start()

        @pl.when(tgt != a)
        def _(q=q):
            piece(q, c).start()

        @pl.when(tgt == a)
        def _(q=q):
            pltpu.make_async_copy(
                proj.at[0, c, 0, pl.ds(q * kc, kc)], arr.at[q, slot], arr_sem.at[q]
            ).start()

    sys_copy.wait()
    first_copy.wait()


    def build(p, carry):
        rows_p = pl.ds(pl.multiple_of(p * W, W), W)
        for g in range(blocks):
            f = first[g, p]
            w = [sysv[g, p, j].astype(jnp.float32) for j in range(2)]
            r = [pltpu.roll(x, W, 1) for x in w]
            up = (lax.broadcasted_iota(jnp.int32, (W, PW), 1) // W)
            for t in range(PW // W):
                x = [jnp.where(up == t, w[j], r[j]) for j in range(2)]
                for h in range(half):
                    b = up + h * (PW // W)
                    second = lax.rem(f + 1, ntiles)
                    tile = jnp.where(b == f, x[0], jnp.where(b == second, x[1], 0.0))
                    A[g * (PW // W) + t, rows_p, pl.ds(h * PW, PW)] = tile.astype(jnp.bfloat16)
        return carry

    lax.fori_loop(0, ptiles, build, 0)

    colp[...] = jnp.zeros_like(colp)
    for cp in img_copies:
        cp.wait()

    def project(t, carry):
        m = A[t]
        F[t] = jnp.dot(
            img[...].reshape(NC * rows, npix), m, preferred_element_type=jnp.float32
        )
        ones_r = jnp.ones((16, npix), jnp.bfloat16)
        ones_b = jnp.ones((16, bins), jnp.bfloat16)
        inv[t] = 1.0 / jnp.dot(ones_r, m, preferred_element_type=jnp.float32)[:8]
        for g in range(G):
            colp[g] += lax.dot_general(
                ones_b, A[t, pl.ds(g * share, share)], NT, preferred_element_type=jnp.float32
            )[:8]
        return carry

    lax.fori_loop(0, T, project, 0)

    for s in range(1, G):
        g = lax.rem(a + s, G)
        pltpu.make_async_remote_copy(
            src_ref=colp.at[g], dst_ref=crecv.at[s - 1], send_sem=csend_sem.at[s - 1],
            recv_sem=crecv_sem, device_id=(c, g), device_id_type=MESH,
        ).start()

    def res_copies(q):
        out = []
        for b in range(G):
            out.append(pltpu.make_async_copy(
                R.at[q, :, b], res_out.at[:, pl.ds(b * KR + q * kc, kc)], res_sem.at[q, b]
            ))
        return out

    def new_copies(q):
        return [
            pltpu.make_async_copy(
                newv.at[q, b], new_out.at[pl.ds(b * KR + q * kc, kc)], new_sem.at[q, b]
            )
            for b in range(G)
        ]

    def residual_part(q):
        def body(t, carry):
            scale = inv[t][:1]
            for b in range(G):
                value = arr[q, b * T + t].astype(jnp.float32)
                f = F[t, pl.ds(q * rows + b * kc, kc)]
                R[q, t, b] = ((value - f) * scale).astype(jnp.bfloat16)
            return carry

        lax.fori_loop(0, T, body, 0)

    def back(q, g):
        total = jnp.zeros((rows, share), jnp.float32)
        pix = pl.ds(pl.multiple_of(g * share, share), share)
        for t in range(T):
            total = total + lax.dot_general(
                R[q, t].reshape(rows, bins), A[t, pix], NT, preferred_element_type=jnp.float32
            )
        return total

    def u_copy(q, s):
        g = lax.rem(a + s, G)
        return pltpu.make_async_remote_copy(
            src_ref=U.at[q, s - 1], dst_ref=urecv.at[q, s - 1],
            send_sem=usend_sem.at[q, s - 1], recv_sem=urecv_sem.at[q, s - 1],
            device_id=(c, g), device_id_type=MESH,
        )

    def process(q):
        pltpu.make_async_copy(arr.at[q], arr.at[q], arr_sem.at[q]).wait()
        residual_part(q)
        for cp in res_copies(q):
            cp.start()
        for s in range(1, G):
            U[q, s - 1] = back(q, lax.rem(a + s, G))
            u_copy(q, s).start()
        own[q] = back(q, a)

    def finish(q):
        total = own[q]
        for s in range(1, G):
            u_copy(q, s).wait_recv()
            total = total + urecv[q, s - 1]
        mine = img[q, :, :, pl.ds(pl.multiple_of(a * share, share), share)]
        new = mine.reshape(rows, share).astype(jnp.float32) + total * own_inv
        newv[q] = new.reshape(G, kc, share)
        for cp in new_copies(q):
            cp.start()

    pltpu.make_async_copy(crecv, crecv, crecv_sem).wait()
    columns = colp[a][:1]
    for s in range(1, G):
        columns = columns + crecv[s - 1][:1]
    own_inv = 1.0 / columns
    for q in range(NC):
        process(q)
        if q >= 1:
            finish(q - 1)
    finish(NC - 1)

    @pl.when(tgt == a)
    def _():
        sent = proj.at[0, pl.ds(0, C - 1)]
        pltpu.make_async_copy(sent, sent, send_sem).wait()

    @pl.when(tgt != a)
    def _():
        pltpu.make_async_copy(proj.at[0], proj.at[0], send_sem).wait()

    for s in range(1, G):
        pltpu.make_async_remote_copy(
            src_ref=colp.at[0], dst_ref=crecv.at[s - 1], send_sem=csend_sem.at[s - 1],
            recv_sem=crecv_sem, device_id=(c, lax.rem(a + s, G)), device_id_type=MESH,
        ).wait_send()
    for q in range(NC):
        for s in range(1, G):
            u_copy(q, s).wait_send()
        for cp in res_copies(q) + new_copies(q):
            cp.wait()


def on_device(C, G, projections, start_image, system, first_tile):
    T = C // G
    KR = projections.shape[3]
    NC = max(1, min(MAX_CHUNKS, KR // 16))
    kc = KR // NC
    rows = G * kc
    slices, npix = start_image.shape
    bins = projections.shape[4]
    share = npix // G
    bf16, f32 = jnp.bfloat16, jnp.float32
    dma = pltpu.SemaphoreType.DMA
    hbm = pl.BlockSpec(memory_space=pl.ANY)
    return pl.pallas_call(
        functools.partial(kernel, C, G, NC),
        out_shape=(
            jax.ShapeDtypeStruct((slices, share), f32),
            jax.ShapeDtypeStruct((T, slices, bins), bf16),
        ),
        in_specs=[pl.BlockSpec(memory_space=pltpu.HBM)] * 4,
        out_specs=(hbm, hbm),
        scratch_shapes=[
            pltpu.SMEM(first_tile.shape, jnp.int32),
            pltpu.VMEM((NC, G, kc, npix), bf16),
            pltpu.VMEM(system.shape, bf16),
            pltpu.VMEM((T, npix, bins), bf16),
            pltpu.VMEM((T, NC * rows, bins), f32),
            pltpu.VMEM((T, 8, bins), f32),
            pltpu.VMEM((NC, C, kc, bins), bf16),
            pltpu.VMEM((NC, T, G, kc, bins), bf16),
            pltpu.VMEM((NC, G - 1, rows, share), f32),
            pltpu.VMEM((NC, rows, share), f32),
            pltpu.VMEM((NC, G - 1, rows, share), f32),
            pltpu.VMEM((G, 8, share), f32),
            pltpu.VMEM((G - 1, 8, share), f32),
            pltpu.VMEM((NC, G, kc, share), f32),
            dma,
            dma((NC, G)),
            dma,
            dma,
            dma((NC,)),
            dma((NC, G - 1)),
            dma((NC, G - 1)),
            dma((G - 1,)),
            dma,
            dma((NC, G)),
            dma((NC, G)),
        ],
        compiler_params=pltpu.CompilerParams(
            collective_id=0, has_side_effects=True, vmem_limit_bytes=63 * 1024 * 1024
        ),
    )(first_tile, projections, start_image, system)


def solution(mesh):
    in_specs = (
        P("cuts", None, "ang", None, None),
        P("cuts", None),
        P("ang", None, None, None, None),
        P("ang", None),
    )
    out_specs = (P("cuts", "ang"), P("ang", "cuts", None))
    return jax.shard_map(
        functools.partial(on_device, mesh.shape["cuts"], mesh.shape["ang"]),
        mesh=mesh, in_specs=in_specs, out_specs=out_specs, check_vma=False,
    )
```

```python
import functools

import jax
import jax.numpy as jnp
from jax import lax
from jax.experimental import pallas as pl
from jax.experimental.pallas import tpu as pltpu
from jax.sharding import PartitionSpec as P

MESH = pl.DeviceIdType.MESH
NT = (((1,), (1,)), ((), ()))
SPLIT = (3, 3, 2)
VMEM_BYTES = 67043328 - 0


def kernel(
    C, G, sizes, first_in, proj, image, system, new_out, res_out,
    first, img, sysv, A, F, inv, arr, R, U, own, urecv, colp, crecv,
    first_sem, img_sem, sys_sem, send_sem, arr_sem,
    usend_sem, urecv_sem, csend_sem, crecv_sem,
):
    c = lax.axis_index("cuts")
    a = lax.axis_index("ang")
    T = C // G
    blocks, ptiles, _, W, PW = system.shape
    KR = proj.shape[3]
    NC = len(sizes)
    starts = [sum(sizes[:q]) for q in range(NC)]
    npix = image.shape[1]
    share = npix // G
    bins = proj.shape[4]
    half = bins // PW
    ntiles = bins // W

    tgt = c // T
    slot = a * T + lax.rem(c, T)

    barrier = pltpu.get_barrier_semaphore()
    for i in range(T):
        source = a * T + lax.rem(c + i, T)
        for s in range(1 if i == 0 else 0, G):
            pl.semaphore_signal(
                barrier, inc=1, device_id=(source, lax.rem(a + s, G)), device_id_type=MESH
            )

    @pl.when(tgt != a)
    def _():
        pl.semaphore_signal(
            barrier, inc=1, device_id=(a * T + lax.rem(c, T), a), device_id_type=MESH
        )

    for s in range(1, G):
        pl.semaphore_signal(barrier, inc=1, device_id=(c, lax.rem(a + s, G)), device_id_type=MESH)

    sys_copy = pltpu.make_async_copy(system, sysv, sys_sem)
    sys_copy.start()
    first_copy = pltpu.make_async_copy(first_in, first, first_sem)
    first_copy.start()
    img_copies = []
    for q in range(NC):
        for b in range(G):
            cp = pltpu.make_async_copy(
                image.at[pl.ds(b * KR + starts[q], sizes[q])],
                img.at[pl.ds(G * starts[q] + b * sizes[q], sizes[q])],
                img_sem.at[q, b],
            )
            cp.start()
            img_copies.append(cp)
    pl.semaphore_wait(barrier, C + G - 1 - jnp.where(tgt == a, 1, 0))

    def piece(q, o):
        return pltpu.make_async_remote_copy(
            src_ref=proj.at[0, o, 0, pl.ds(starts[q], sizes[q])],
            dst_ref=arr[q].at[slot],
            send_sem=send_sem,
            recv_sem=arr_sem.at[q],
            device_id=(o, tgt),
            device_id_type=MESH,
        )

    for q in range(NC):
        for s in range(1, C):
            piece(q, lax.rem(c + s, C)).start()

        @pl.when(tgt != a)
        def _(q=q):
            piece(q, c).start()

        @pl.when(tgt == a)
        def _(q=q):
            pltpu.make_async_copy(
                proj.at[0, c, 0, pl.ds(starts[q], sizes[q])], arr[q].at[slot], arr_sem.at[q]
            ).start()

    sys_copy.wait()
    first_copy.wait()


    def build(p, carry):
        rows_p = pl.ds(pl.multiple_of(p * W, W), W)
        for g in range(blocks):
            f = first[g, p]
            w = [sysv[g, p, j].astype(jnp.float32) for j in range(2)]
            r = [pltpu.roll(x, W, 1) for x in w]
            up = (lax.broadcasted_iota(jnp.int32, (W, PW), 1) // W)
            for t in range(PW // W):
                x = [jnp.where(up == t, w[j], r[j]) for j in range(2)]
                for h in range(half):
                    b = up + h * (PW // W)
                    second = lax.rem(f + 1, ntiles)
                    tile = jnp.where(b == f, x[0], jnp.where(b == second, x[1], 0.0))
                    A[g * (PW // W) + t, rows_p, pl.ds(h * PW, PW)] = tile.astype(jnp.bfloat16)
        return carry

    lax.fori_loop(0, ptiles, build, 0)

    colp[...] = jnp.zeros_like(colp)
    for cp in img_copies:
        cp.wait()

    def project(t, carry):
        m = A[t]
        F[t] = jnp.dot(
            img[...], m, preferred_element_type=jnp.float32
        )
        ones_r = jnp.ones((16, npix), jnp.bfloat16)
        ones_b = jnp.ones((16, bins), jnp.bfloat16)
        inv[t] = 1.0 / jnp.dot(ones_r, m, preferred_element_type=jnp.float32)[:8]
        for g in range(G):
            colp[g] += lax.dot_general(
                ones_b, A[t, pl.ds(g * share, share)], NT, preferred_element_type=jnp.float32
            )[:8]
        return carry

    lax.fori_loop(0, T, project, 0)

    for s in range(1, G):
        g = lax.rem(a + s, G)
        pltpu.make_async_remote_copy(
            src_ref=colp.at[g], dst_ref=crecv.at[s - 1], send_sem=csend_sem.at[s - 1],
            recv_sem=crecv_sem, device_id=(c, g), device_id_type=MESH,
        ).start()

    def residual_part(q):
        def body(t, carry):
            scale = inv[t][:1]
            for b in range(G):
                value = arr[q][b * T + t].astype(jnp.float32)
                f = F[t, pl.ds(G * starts[q] + b * sizes[q], sizes[q])]
                res = ((value - f) * scale).astype(jnp.bfloat16)
                R[q][t, pl.ds(b * sizes[q], sizes[q])] = res
                res_out[t, pl.ds(b * KR + starts[q], sizes[q])] = res
            return carry

        lax.fori_loop(0, T, body, 0)

    def back(q, g):
        total = jnp.zeros((G * sizes[q], share), jnp.float32)
        pix = pl.ds(pl.multiple_of(g * share, share), share)
        for t in range(T):
            total = total + lax.dot_general(
                R[q][t], A[t, pix], NT, preferred_element_type=jnp.float32
            )
        return total

    def u_copy(q, s):
        g = lax.rem(a + s, G)
        return pltpu.make_async_remote_copy(
            src_ref=U[q].at[s - 1], dst_ref=urecv[q].at[s - 1],
            send_sem=usend_sem.at[q, s - 1], recv_sem=urecv_sem.at[q, s - 1],
            device_id=(c, g), device_id_type=MESH,
        )

    def process(q):
        pltpu.make_async_copy(arr[q], arr[q], arr_sem.at[q]).wait()
        residual_part(q)
        for s in range(1, G):
            U[q][s - 1] = back(q, lax.rem(a + s, G))
            u_copy(q, s).start()
        own[q][...] = back(q, a)

    def finish(q):
        total = own[q][...]
        for s in range(1, G):
            u_copy(q, s).wait_recv()
            total = total + urecv[q][s - 1]
        mine = img[
            pl.ds(G * starts[q], G * sizes[q]), pl.ds(pl.multiple_of(a * share, share), share)
        ]
        new = mine.astype(jnp.float32) + total * own_inv
        for b in range(G):
            new_out[pl.ds(b * KR + starts[q], sizes[q])] = new[b * sizes[q] : (b + 1) * sizes[q]]

    pltpu.make_async_copy(crecv, crecv, crecv_sem).wait()
    columns = colp[a][:1]
    for s in range(1, G):
        columns = columns + crecv[s - 1][:1]
    own_inv = 1.0 / columns
    for q in range(NC):
        process(q)
        if q >= 1:
            finish(q - 1)
    finish(NC - 1)

    @pl.when(tgt == a)
    def _():
        sent = proj.at[0, pl.ds(0, C - 1)]
        pltpu.make_async_copy(sent, sent, send_sem).wait()

    @pl.when(tgt != a)
    def _():
        pltpu.make_async_copy(proj.at[0], proj.at[0], send_sem).wait()

    for s in range(1, G):
        pltpu.make_async_remote_copy(
            src_ref=colp.at[0], dst_ref=crecv.at[s - 1], send_sem=csend_sem.at[s - 1],
            recv_sem=crecv_sem, device_id=(c, lax.rem(a + s, G)), device_id_type=MESH,
        ).wait_send()
    for q in range(NC):
        for s in range(1, G):
            u_copy(q, s).wait_send()


def chunk_sizes(rows):
    unit = max(16, rows // sum(SPLIT))
    sizes = [n * unit for n in SPLIT]
    if sum(sizes) == rows:
        return sizes
    return [16] * (rows // 16) if rows % 16 == 0 else [rows]


def on_device(C, G, projections, start_image, system, first_tile):
    T = C // G
    KR = projections.shape[3]
    sizes = chunk_sizes(KR)
    NC = len(sizes)
    slices, npix = start_image.shape
    bins = projections.shape[4]
    share = npix // G
    bf16, f32 = jnp.bfloat16, jnp.float32
    dma = pltpu.SemaphoreType.DMA
    out_bytes = slices * share * 4 + T * slices * bins * 2
    return pl.pallas_call(
        functools.partial(kernel, C, G, sizes),
        out_shape=(
            pltpu.VMEM((slices, share), f32),
            pltpu.VMEM((T, slices, bins), bf16),
        ),
        in_specs=[pl.BlockSpec(memory_space=pltpu.HBM)] * 4,
        out_specs=(pl.BlockSpec(memory_space=pltpu.VMEM),) * 2,
        scratch_shapes=[
            pltpu.SMEM(first_tile.shape, jnp.int32),
            pltpu.VMEM((slices, npix), bf16),
            pltpu.VMEM(system.shape, bf16),
            pltpu.VMEM((T, npix, bins), bf16),
            pltpu.VMEM((T, slices, bins), f32),
            pltpu.VMEM((T, 8, bins), f32),
            [pltpu.VMEM((C, n, bins), bf16) for n in sizes],
            [pltpu.VMEM((T, G * n, bins), bf16) for n in sizes],
            [pltpu.VMEM((G - 1, G * n, share), f32) for n in sizes],
            [pltpu.VMEM((G * n, share), f32) for n in sizes],
            [pltpu.VMEM((G - 1, G * n, share), f32) for n in sizes],
            pltpu.VMEM((G, 8, share), f32),
            pltpu.VMEM((G - 1, 8, share), f32),
            dma,
            dma((NC, G)),
            dma,
            dma,
            dma((NC,)),
            dma((NC, G - 1)),
            dma((NC, G - 1)),
            dma((G - 1,)),
            dma,
        ],
        compiler_params=pltpu.CompilerParams(
            collective_id=0, has_side_effects=True, vmem_limit_bytes=VMEM_BYTES - out_bytes
        ),
    )(first_tile, projections, start_image, system)


def solution(mesh):
    in_specs = (
        P("cuts", None, "ang", None, None),
        P("cuts", None),
        P("ang", None, None, None, None),
        P("ang", None),
    )
    out_specs = (P("cuts", "ang"), P("ang", "cuts", None))
    return jax.shard_map(
        functools.partial(on_device, mesh.shape["cuts"], mesh.shape["ang"]),
        mesh=mesh, in_specs=in_specs, out_specs=out_specs, check_vma=False,
    )
```

```python
import functools

import jax
import jax.numpy as jnp
from jax import lax
from jax.experimental import pallas as pl
from jax.experimental.pallas import tpu as pltpu
from jax.sharding import PartitionSpec as P

MESH = pl.DeviceIdType.MESH
NT = (((1,), (1,)), ((), ()))
SPLIT = (3, 3, 2)
PUTS = 4
VMEM_BYTES = 67043328 - 0


def kernel(
    C, G, sizes, first_in, proj, image, system, new_out, res_out,
    first, img, sysv, A, F, inv, arr, R, U, own, urecv, colp, crecv,
    first_sem, img_sem, sys_sem, send_sem, arr_sem,
    usend_sem, urecv_sem, csend_sem, crecv_sem,
):
    c = lax.axis_index("cuts")
    a = lax.axis_index("ang")
    T = C // G
    blocks, ptiles, _, W, PW = system.shape
    KR = proj.shape[3]
    NC = len(sizes)
    starts = [sum(sizes[:q]) for q in range(NC)]
    npix = image.shape[1]
    share = npix // G
    bins = proj.shape[4]
    half = bins // PW
    ntiles = bins // W

    tgt = c // T
    slot = a * T + lax.rem(c, T)

    barrier = pltpu.get_barrier_semaphore()
    for i in range(T):
        source = a * T + lax.rem(c + i, T)
        for s in range(1 if i == 0 else 0, G):
            pl.semaphore_signal(
                barrier, inc=1, device_id=(source, lax.rem(a + s, G)), device_id_type=MESH
            )

    @pl.when(tgt != a)
    def _():
        pl.semaphore_signal(
            barrier, inc=1, device_id=(a * T + lax.rem(c, T), a), device_id_type=MESH
        )

    for s in range(1, G):
        pl.semaphore_signal(barrier, inc=1, device_id=(c, lax.rem(a + s, G)), device_id_type=MESH)

    sys_copy = pltpu.make_async_copy(system, sysv, sys_sem)
    sys_copy.start()
    first_copy = pltpu.make_async_copy(first_in, first, first_sem)
    first_copy.start()
    img_copies = []
    for q in range(NC):
        for b in range(G):
            cp = pltpu.make_async_copy(
                image.at[pl.ds(b * KR + starts[q], sizes[q])],
                img.at[pl.ds(G * starts[q] + b * sizes[q], sizes[q])],
                img_sem.at[q, b],
            )
            cp.start()
            img_copies.append(cp)
    pl.semaphore_wait(barrier, C + G - 1 - jnp.where(tgt == a, 1, 0))

    def piece(q, o):
        return pltpu.make_async_remote_copy(
            src_ref=proj.at[0, o, 0, pl.ds(starts[q], sizes[q])],
            dst_ref=arr[q].at[slot],
            send_sem=send_sem,
            recv_sem=arr_sem.at[q],
            device_id=(o, tgt),
            device_id_type=MESH,
        )

    for q in range(NC):
        for s in range(1, C):
            piece(q, lax.rem(c + s, C)).start()

        @pl.when(tgt != a)
        def _(q=q):
            piece(q, c).start()

        @pl.when(tgt == a)
        def _(q=q):
            pltpu.make_async_copy(
                proj.at[0, c, 0, pl.ds(starts[q], sizes[q])], arr[q].at[slot], arr_sem.at[q]
            ).start()

    sys_copy.wait()
    first_copy.wait()


    def build(p, carry):
        rows_p = pl.ds(pl.multiple_of(p * W, W), W)
        for g in range(blocks):
            f = first[g, p]
            w = [sysv[g, p, j].astype(jnp.float32) for j in range(2)]
            r = [pltpu.roll(x, W, 1) for x in w]
            up = (lax.broadcasted_iota(jnp.int32, (W, PW), 1) // W)
            for t in range(PW // W):
                x = [jnp.where(up == t, w[j], r[j]) for j in range(2)]
                for h in range(half):
                    b = up + h * (PW // W)
                    second = lax.rem(f + 1, ntiles)
                    tile = jnp.where(b == f, x[0], jnp.where(b == second, x[1], 0.0))
                    A[g * (PW // W) + t, rows_p, pl.ds(h * PW, PW)] = tile.astype(jnp.bfloat16)
        return carry

    lax.fori_loop(0, ptiles, build, 0)

    colp[...] = jnp.zeros_like(colp)
    for cp in img_copies:
        cp.wait()

    def project(t, carry):
        m = A[t]
        F[t] = jnp.dot(
            img[...], m, preferred_element_type=jnp.float32
        )
        ones_r = jnp.ones((16, npix), jnp.bfloat16)
        ones_b = jnp.ones((16, bins), jnp.bfloat16)
        inv[t] = 1.0 / jnp.dot(ones_r, m, preferred_element_type=jnp.float32)[:8]
        for g in range(G):
            colp[g] += lax.dot_general(
                ones_b, A[t, pl.ds(g * share, share)], NT, preferred_element_type=jnp.float32
            )[:8]
        return carry

    lax.fori_loop(0, T, project, 0)

    for s in range(1, G):
        g = lax.rem(a + s, G)
        pltpu.make_async_remote_copy(
            src_ref=colp.at[g], dst_ref=crecv.at[s - 1], send_sem=csend_sem.at[s - 1],
            recv_sem=crecv_sem, device_id=(c, g), device_id_type=MESH,
        ).start()

    def residual_part(q):
        def body(t, carry):
            scale = inv[t][:1]
            for b in range(G):
                value = arr[q][b * T + t].astype(jnp.float32)
                f = F[t, pl.ds(G * starts[q] + b * sizes[q], sizes[q])]
                res = ((value - f) * scale).astype(jnp.bfloat16)
                R[q][t, pl.ds(b * sizes[q], sizes[q])] = res
                res_out[t, pl.ds(b * KR + starts[q], sizes[q])] = res
            return carry

        lax.fori_loop(0, T, body, 0)

    def back(q, g):
        total = jnp.zeros((G * sizes[q], share), jnp.float32)
        pix = pl.ds(pl.multiple_of(g * share, share), share)
        for t in range(T):
            total = total + lax.dot_general(
                R[q][t], A[t, pix], NT, preferred_element_type=jnp.float32
            )
        return total

    def u_copy(q, s):
        g = lax.rem(a + s, G)
        return pltpu.make_async_remote_copy(
            src_ref=U[q].at[s - 1], dst_ref=urecv[q].at[s - 1],
            send_sem=usend_sem.at[q, s - 1], recv_sem=urecv_sem.at[q, s - 1],
            device_id=(c, g), device_id_type=MESH,
        )

    def process(q):
        pltpu.make_async_copy(arr[q], arr[q], arr_sem.at[q]).wait()
        residual_part(q)
        for s in range(1, G):
            U[q][s - 1] = back(q, lax.rem(a + s, G))
            u_copy(q, s).start()
        own[q][...] = back(q, a)

    def finish(q):
        total = own[q][...]
        for s in range(1, G):
            u_copy(q, s).wait_recv()
            total = total + urecv[q][s - 1]
        mine = img[
            pl.ds(G * starts[q], G * sizes[q]), pl.ds(pl.multiple_of(a * share, share), share)
        ]
        new = mine.astype(jnp.float32) + total * own_inv
        for b in range(G):
            new_out[pl.ds(b * KR + starts[q], sizes[q])] = new[b * sizes[q] : (b + 1) * sizes[q]]

    pltpu.make_async_copy(crecv, crecv, crecv_sem).wait()
    columns = colp[a][:1]
    for s in range(1, G):
        columns = columns + crecv[s - 1][:1]
    own_inv = 1.0 / columns
    for q in range(NC):
        process(q)
        if q >= 1:
            finish(q - 1)
    finish(NC - 1)

    @pl.when(tgt == a)
    def _():
        sent = proj.at[0, pl.ds(0, C - 1)]
        pltpu.make_async_copy(sent, sent, send_sem).wait()

    @pl.when(tgt != a)
    def _():
        pltpu.make_async_copy(proj.at[0], proj.at[0], send_sem).wait()

    for s in range(1, G):
        pltpu.make_async_remote_copy(
            src_ref=colp.at[0], dst_ref=crecv.at[s - 1], send_sem=csend_sem.at[s - 1],
            recv_sem=crecv_sem, device_id=(c, lax.rem(a + s, G)), device_id_type=MESH,
        ).wait_send()
    for q in range(NC):
        for s in range(1, G):
            u_copy(q, s).wait_send()


def put_out(new_in, res_in, new_out, res_out, sem):
    copies = []
    for i, (src, dst) in enumerate(((new_in, new_out), (res_in, res_out))):
        n = src.shape[0] // PUTS
        for k in range(PUTS):
            part = pl.ds(k * n, n)
            copies.append(pltpu.make_async_copy(src.at[part], dst.at[part], sem.at[i * PUTS + k]))
    for cp in copies:
        cp.start()
    for cp in copies:
        cp.wait()


def chunk_sizes(rows):
    unit = max(16, rows // sum(SPLIT))
    sizes = [n * unit for n in SPLIT]
    if sum(sizes) == rows:
        return sizes
    return [16] * (rows // 16) if rows % 16 == 0 else [rows]


def on_device(C, G, projections, start_image, system, first_tile):
    T = C // G
    KR = projections.shape[3]
    sizes = chunk_sizes(KR)
    NC = len(sizes)
    slices, npix = start_image.shape
    bins = projections.shape[4]
    share = npix // G
    bf16, f32 = jnp.bfloat16, jnp.float32
    dma = pltpu.SemaphoreType.DMA
    out_bytes = slices * share * 4 + T * slices * bins * 2
    new_image, residual = pl.pallas_call(
        functools.partial(kernel, C, G, sizes),
        out_shape=(
            pltpu.VMEM((slices, share), f32),
            pltpu.VMEM((T, slices, bins), bf16),
        ),
        in_specs=[pl.BlockSpec(memory_space=pltpu.HBM)] * 4,
        out_specs=(pl.BlockSpec(memory_space=pltpu.VMEM),) * 2,
        scratch_shapes=[
            pltpu.SMEM(first_tile.shape, jnp.int32),
            pltpu.VMEM((slices, npix), bf16),
            pltpu.VMEM(system.shape, bf16),
            pltpu.VMEM((T, npix, bins), bf16),
            pltpu.VMEM((T, slices, bins), f32),
            pltpu.VMEM((T, 8, bins), f32),
            [pltpu.VMEM((C, n, bins), bf16) for n in sizes],
            [pltpu.VMEM((T, G * n, bins), bf16) for n in sizes],
            [pltpu.VMEM((G - 1, G * n, share), f32) for n in sizes],
            [pltpu.VMEM((G * n, share), f32) for n in sizes],
            [pltpu.VMEM((G - 1, G * n, share), f32) for n in sizes],
            pltpu.VMEM((G, 8, share), f32),
            pltpu.VMEM((G - 1, 8, share), f32),
            dma,
            dma((NC, G)),
            dma,
            dma,
            dma((NC,)),
            dma((NC, G - 1)),
            dma((NC, G - 1)),
            dma((G - 1,)),
            dma,
        ],
        compiler_params=pltpu.CompilerParams(
            collective_id=0, has_side_effects=True, vmem_limit_bytes=VMEM_BYTES - out_bytes
        ),
    )(first_tile, projections, start_image, system)
    return pl.pallas_call(
        put_out,
        out_shape=(
            jax.ShapeDtypeStruct(new_image.shape, f32),
            jax.ShapeDtypeStruct(residual.shape, bf16),
        ),
        in_specs=[pl.BlockSpec(memory_space=pl.ANY)] * 2,
        out_specs=(pl.BlockSpec(memory_space=pl.ANY),) * 2,
        scratch_shapes=[dma((2 * PUTS,))],
        compiler_params=pltpu.CompilerParams(vmem_limit_bytes=1 << 20),
    )(new_image, residual)


def solution(mesh):
    in_specs = (
        P("cuts", None, "ang", None, None),
        P("cuts", None),
        P("ang", None, None, None, None),
        P("ang", None),
    )
    out_specs = (P("cuts", "ang"), P("ang", "cuts", None))
    return jax.shard_map(
        functools.partial(on_device, mesh.shape["cuts"], mesh.shape["ang"]),
        mesh=mesh, in_specs=in_specs, out_specs=out_specs, check_vma=False,
    )
```
